32 devices in a mesh: section: 2 (over y), expert: 16 (over z, x, core).
Axes of the slice: x: 2, y: 2, z: 4, core: 2. Of those that a mesh axis runs over, the one named last changes fastest.
Arguments:
- tokens: bfloat16 [2048, 7168], P('expert', 'section'), may hold values from -6 to 6
- exponents: int32 [2048, 56], P('expert', 'section'), may hold values from -9 to -5
- expert_ids: int32 [2048, 8], P('expert'), may hold values from 0 to 15, all different within a row; in each aligned block of 128 rows (0 to 127, 128 to 255, ...) at most 80 rows name the same one
- affinity: float32 [2048, 8], P('expert'), may hold values from 0.1 to 1
- w_gate: bfloat16 [16, 7168, 2048], P('expert', None, 'section'), may hold values from -0.0625 to 0.0625
- w_up: bfloat16 [16, 7168, 2048], P('expert', None, 'section'), may hold values from -0.0625 to 0.0625
- w_down: bfloat16 [16, 2048, 7168], P('expert', 'section'), may hold values from -0.125 to 0.125
Outputs:
- moe_out: bfloat16 [2048, 7168], P('expert', 'section')
The draws below stay inside these ranges and needn't reach their ends.
Inputs may be any that keep to these rules, and one draw needn't show every extreme that they name: `expert_ids`: each row names 8 different experts. In the 128 rows of one token group no expert is named more than 80 times, a bound that some block reaches.
All inputs are finite; a program needn't handle non-finite values.
Results may differ from the reference program's by a relative error of at most 0.012.
Values may be sent and summed in bfloat16 or wider, within the bound.
No kernel may reach another device: no remote copies, remote signals or barrier semaphores. Data moves between devices by JAX's collectives and lax.ppermute only.
A program may use at most 192 MiB of HBM per device.

```python
import math
import jax
import jax.numpy as jnp
import numpy as np
from jax import lax

D = 7168
FF = 2048
TOPK = 8
TOK_DEV = 128
EXPERTS = 16
TOKENS = 2048
CAP = 80
N_SECTION = 2
N_EXPERT = 16


def set_ends(array, rng, least, top_value):
    dims = array.shape
    index_at = [jax.random.randint(jax.random.fold_in(rng, axis), (), 0, dims[axis]) for axis in range(len(dims))]
    array = array.at[tuple(index_at)].set(least)
    longest = dims.index(max(dims))
    index_at[longest] = (index_at[longest] + 1) % dims[longest]
    return array.at[tuple(index_at)].set(top_value)


def block_levels(key, shape, pieces, smallest, top_value):
    level = 1.0
    for dim, parts in pieces:
        draws = jax.random.uniform(jax.random.fold_in(jax.random.fold_in(key, 6), dim), (parts,), jnp.float32, smallest / len(pieces), top_value / len(pieces))
        level = level * jnp.repeat(jnp.exp(draws), shape[dim] // parts).reshape((-1,) + (1,) * (len(shape) - 1 - dim))
    return level


def shared_out(stream_key, own, number, rows, number_of, top, most, lean):
    ranking = jax.random.permutation(stream_key, number_of)
    heavy_load, ordinary = portions_of(number_of, rows * top, most, lean, True), portions_of(number_of, rows * top, most, lean, False)
    places = jnp.arange(number_of)

    def named(sizes, turn):
        used = int((sizes > 0).sum())
        fixed = max(1, used // 4)
        shifted = fixed + (places - fixed + turn * (used - fixed)) % max(1, number_of - fixed)
        return jnp.zeros((number_of,), jnp.int32).at[ranking[jnp.where(places < fixed, places, shifted)]].set(jnp.asarray(sizes, jnp.int32))

    sizes = jnp.where(number % 4 == 0, named(heavy_load, number // 4), named(ordinary, number - number // 4 - 1))
    mixed = jax.random.permutation(jax.random.fold_in(own, 3), number_of)
    giver, sink = mixed[0:number_of // 2 * 2:2], mixed[1:number_of // 2 * 2:2]
    margin = jnp.minimum(sizes[giver] - 1, most - sizes[sink]) // 2
    margin = jnp.where((giver == ranking[0]) | (sink == ranking[0]) | (sizes[sink] == 0), 0, jnp.maximum(margin, 0))
    shifted = jax.random.randint(jax.random.fold_in(own, 4), (number_of // 2,), 0, 1 << 20) % (margin + 1)
    sizes = sizes.at[giver].add(-shifted).at[sink].add(shifted)
    members = jnp.searchsorted(jnp.cumsum(sizes), jnp.arange(rows * top), side="right").astype(jnp.int32)
    table = members.reshape(top, rows).T
    table = table[jax.random.permutation(jax.random.fold_in(own, 1), rows)]
    turn = jax.random.randint(jax.random.fold_in(own, 2), (rows, 1), 0, top)
    return jnp.take_along_axis(table, (jnp.arange(top)[None, :] + turn) % top, axis=1)


def portions_of(number_of, total, bound, skew, full):
    loads = [(1 << 20) // math.isqrt(grade ** skew) + 1 for grade in range(1, number_of + 1)]
    largest = bound if full else min(bound, max(-(-total // number_of), total * loads[0] // sum(loads)))
    least = 1 if total - largest >= number_of - 1 else 0
    given, surplus = [largest] + [least] * (number_of - 1), total - largest - least * (number_of - 1)
    while surplus > 0:
        free = [i for i in range(1, number_of) if given[i] < largest] or [i for i in range(1, number_of) if given[i] < bound]
        whole, budget = sum([loads[i] for i in free]), surplus
        for i in free:
            addition = min(bound - given[i], max(1, budget * loads[i] // whole), surplus)
            given[i] = given[i] + addition
            surplus = surplus - addition
    return np.array(given)


def noise(own_key, shape, scale, reach, shards=(), kind=jnp.bfloat16):
    entries = scale * jax.random.normal(own_key, shape, jnp.float32)
    if shards:
        entries = entries * block_levels(own_key, shape, shards, -0.22, 0.18)
    return jnp.clip(entries, -reach, reach).astype(kind)


def setup_inputs(seed: int = 0) -> dict:
    keys = jax.random.split(jax.random.key(seed), 8)
    tokens = noise(keys[0], (TOKENS, D), 1.0, 6.0, ((0, 16), (1, 2)))
    exponents = set_ends(jax.random.randint(keys[1], (TOKENS, D // 128), -9, -4), jax.random.fold_in(keys[1], 1), -9, (-4) - 1).astype(jnp.int32)
    expert_ids_keys = jax.random.split(jax.random.fold_in(keys[2], 1), TOKENS // TOK_DEV)
    expert_ids_turns = jax.random.permutation(jax.random.fold_in(keys[2], 3), TOKENS // TOK_DEV)
    expert_ids = jax.vmap(lambda own, number: shared_out(jax.random.fold_in(keys[2], 2), own, number, TOK_DEV, EXPERTS, TOPK, CAP, 2))(expert_ids_keys, expert_ids_turns).reshape((TOKENS, TOPK))
    affinity = jnp.clip(jnp.exp(math.log(1.0) - 2.3025851 * jax.random.uniform(keys[3], (TOKENS, TOPK), jnp.float32) ** block_levels(keys[3], (TOKENS, TOPK), ((0, 16),), -0.2, 0.2)), 0.1, 1.0)
    w_gate = noise(keys[4], (EXPERTS, D, FF), D ** -0.5, 0.0625, ((0, 16), (2, 2)))
    w_up = noise(keys[5], (EXPERTS, D, FF), D ** -0.5, 0.0625, ((0, 16), (2, 2)))
    w_down = noise(keys[6], (EXPERTS, FF, D), FF ** -0.5, 0.125, ((0, 16), (1, 2)))
    return dict(tokens=tokens, exponents=exponents, expert_ids=expert_ids, affinity=affinity, w_gate=w_gate, w_up=w_up, w_down=w_down)


quant_limit = 448.0
route_scaling = 2.5


def slot_positions(ids, capacity, experts):
    flat = ids.reshape(-1).astype(jnp.int32)
    marks = (flat[:, None] == jnp.arange(experts, dtype=jnp.int32)[None, :]).astype(jnp.int32)
    before = jnp.cumsum(marks, axis=0).astype(jnp.int32) - marks
    slot = jnp.sum(before * marks, axis=1).astype(jnp.int32)
    return (flat * capacity + slot).reshape(ids.shape).astype(jnp.int32)


def reference(tokens, exponents, expert_ids, affinity, w_gate, w_up, w_down):
    groups = N_EXPERT
    scales = jnp.exp2(exponents.astype(jnp.float32))
    tiles = tokens.astype(jnp.float32).reshape(TOKENS, D // 128, 128) / scales[:, :, None]
    quant = jnp.clip(tiles, -quant_limit, quant_limit).astype(jnp.bfloat16)
    restored = (quant.astype(jnp.float32) * scales[:, :, None]).astype(jnp.bfloat16).reshape(TOKENS, D)
    group_rows = restored.reshape(groups, TOK_DEV, D)
    group_ids = expert_ids.reshape(groups, TOK_DEV, TOPK)
    positions = jax.vmap(lambda ids: slot_positions(ids, CAP, EXPERTS))(group_ids)

    def fill(rows, where):
        source = jnp.repeat(rows, TOPK, axis=0)
        empty = jnp.zeros((EXPERTS * CAP, D), jnp.bfloat16)
        return empty.at[where.reshape(-1)].set(source)

    buffers = jax.vmap(fill)(group_rows, positions)
    by_expert = buffers.reshape(groups, EXPERTS, CAP, D).transpose(1, 0, 2, 3)
    quarter = FF // N_SECTION

    def run_expert(operands):
        inputs, gate_w, up_w, down_w = operands
        rows = inputs.reshape(groups * CAP, D).astype(jnp.float32)
        gate = jnp.dot(rows, gate_w.astype(jnp.float32))
        up = jnp.dot(rows, up_w.astype(jnp.float32))
        hidden = (jax.nn.silu(gate) * up).astype(jnp.bfloat16)
        total = jnp.zeros((groups * CAP, D), jnp.float32)
        for part in range(N_SECTION):
            piece = jnp.dot(hidden[:, part * quarter:(part + 1) * quarter].astype(jnp.float32),
                            down_w[part * quarter:(part + 1) * quarter].astype(jnp.float32))
            total = total + piece.astype(jnp.bfloat16).astype(jnp.float32)
        return total.astype(jnp.bfloat16).reshape(groups, CAP, D)

    outputs = lax.map(run_expert, (by_expert, w_gate, w_up, w_down))
    combined = outputs.transpose(1, 0, 2, 3).reshape(groups, EXPERTS * CAP, D)
    route_weight = route_scaling * affinity / jnp.sum(affinity, axis=1, keepdims=True)
    group_weight = route_weight.reshape(groups, TOK_DEV, TOPK)
    total = jnp.zeros((groups, TOK_DEV, D), jnp.float32)
    for choice_index in range(TOPK):
        picked = jax.vmap(lambda rows, where: jnp.take(rows, where, axis=0))(combined, positions[:, :, choice_index])
        total = total + picked.astype(jnp.float32) * group_weight[:, :, choice_index, None]
    return total.reshape(TOKENS, D).astype(jnp.bfloat16)
```

```python
import functools

import jax
import jax.numpy as jnp
from jax import lax
from jax.experimental import pallas as pl
from jax.experimental.pallas import tpu as pltpu
from jax.sharding import PartitionSpec as P


quant_limit = 448.0
route_scaling = 2.5
lane = 128


def restore_kernel(scales_ref, tokens_ref, out_ref):
    for tile in range(tokens_ref.shape[1] // lane):
        span = slice(tile * lane, (tile + 1) * lane)
        scale = scales_ref[:, tile : tile + 1]
        quant = jnp.clip(tokens_ref[:, span].astype(jnp.float32) / scale, -quant_limit, quant_limit)
        restored = quant.astype(jnp.bfloat16).astype(jnp.float32) * scale
        out_ref[:, span] = restored.astype(jnp.bfloat16)


def restore(tokens, scales):
    return pl.pallas_call(
        restore_kernel,
        out_shape=jax.ShapeDtypeStruct(tokens.shape, jnp.bfloat16),
        cost_estimate=pl.CostEstimate(
            flops=4 * tokens.size, bytes_accessed=4 * tokens.size, transcendentals=0
        ),
        name="restore",
    )(scales, tokens)


def up_kernel(units, cap, side_ref, pick_ref, weight_ref, *refs):
    mine, theirs = refs[:units], refs[units : 2 * units]
    gate_ref, up_ref, hidden_ref, rows_ref, gate_sum, up_sum = refs[2 * units :]
    step = pl.program_id(0)
    part = pl.program_id(1)
    side = side_ref[0]

    @pl.when((step == 0) & (part == 0))
    def _():
        for unit in range(units):
            span = slice(unit * cap, (unit + 1) * cap)
            for source, place in ((mine[unit], side), (theirs[unit], 1 - side)):
                rows_ref[place, span, :] = jnp.dot(
                    pick_ref[unit], source[...], preferred_element_type=jnp.float32
                ).astype(jnp.bfloat16)

    @pl.when(part == 0)
    def _():
        gate_sum[...] = jnp.zeros_like(gate_sum)
        up_sum[...] = jnp.zeros_like(up_sum)

    rows = rows_ref[part]
    gate_sum[...] += jnp.dot(rows, gate_ref[...], preferred_element_type=jnp.float32)
    up_sum[...] += jnp.dot(rows, up_ref[...], preferred_element_type=jnp.float32)

    @pl.when(part == 1)
    def _():
        gate = gate_sum[...]
        hidden = gate / (1.0 + jnp.exp(-gate)) * up_sum[...] * weight_ref[...]
        hidden_ref[...] = hidden.astype(jnp.bfloat16)


def down_kernel(units, cap, half_steps, side_ref, put_ref, hidden_ref, down_ref, *refs):
    outs, rows_ref = refs[: 2 * units], refs[2 * units]
    step = pl.program_id(0)
    rows_ref[...] = jnp.dot(
        hidden_ref[...], down_ref[...], preferred_element_type=jnp.float32
    ).astype(jnp.bfloat16)

    def finish(targets):
        for unit in range(units):
            targets[unit][...] = jnp.dot(
                put_ref[unit],
                rows_ref[unit * cap : (unit + 1) * cap, :],
                preferred_element_type=jnp.float32,
            ).astype(jnp.bfloat16)

    @pl.when(step < half_steps)
    def _():
        finish(outs[:units])

    @pl.when(step >= half_steps)
    def _():
        finish(outs[units:])


def single(shape):
    return pl.BlockSpec(shape, lambda *_: (0,) * len(shape), pipeline_mode=pl.Buffered(1))


def quarter_of(quarter, shape):
    place = (quarter,) + (0,) * (len(shape) - 1)
    return pl.BlockSpec(shape, lambda *_: place, pipeline_mode=pl.Buffered(1))


def ffn_up(quarter, side, pick, weight, mine, theirs, w_gate, w_up):
    units = len(mine)
    tokens, width = mine[0].shape
    cap = pick.shape[1]
    hidden = w_gate.shape[1]
    wide = 512 if hidden % 512 == 0 else hidden
    rows = units * cap
    tile = pl.BlockSpec((width, wide), lambda n, k, s: (k, n))
    return pl.pallas_call(
        functools.partial(up_kernel, units, cap),
        out_shape=jax.ShapeDtypeStruct((rows, hidden), jnp.bfloat16),
        grid_spec=pltpu.PrefetchScalarGridSpec(
            num_scalar_prefetch=1,
            grid=(hidden // wide, 2),
            in_specs=[quarter_of(quarter, (units, cap, tokens)), quarter_of(quarter, (rows, 1))]
            + [single((tokens, width))] * (2 * units)
            + [tile, tile],
            out_specs=pl.BlockSpec((rows, wide), lambda n, k, s: (0, n)),
            scratch_shapes=[
                pltpu.VMEM((2, rows, width), jnp.bfloat16),
                pltpu.VMEM((rows, wide), jnp.float32),
                pltpu.VMEM((rows, wide), jnp.float32),
            ],
        ),
        compiler_params=pltpu.CompilerParams(dimension_semantics=("arbitrary", "arbitrary")),
        cost_estimate=pl.CostEstimate(
            flops=8 * rows * hidden * width,
            bytes_accessed=8 * hidden * width + 4 * units * tokens * width,
            transcendentals=rows * hidden,
        ),
        name="ffn_up",
    )(side, pick, weight, *mine, *theirs, w_gate, w_up)


def ffn_down(quarter, side, put, hidden_rows, w_down, width):
    _, tokens, cap = put.shape
    rows, hidden = hidden_rows.shape
    units = rows // cap
    half_steps = 2
    tall = width // half_steps

    def down_map(j, s):
        far = j >= half_steps
        return (0, jnp.where(far, (1 - s[0]) * half_steps + j - half_steps, s[0] * half_steps + j))

    out = jax.ShapeDtypeStruct((tokens, width), jnp.bfloat16)
    results = pl.pallas_call(
        functools.partial(down_kernel, units, cap, half_steps),
        out_shape=[out] * (2 * units),
        grid_spec=pltpu.PrefetchScalarGridSpec(
            num_scalar_prefetch=1,
            grid=(2 * half_steps,),
            in_specs=[quarter_of(quarter, (units, tokens, cap)), single(hidden_rows.shape), pl.BlockSpec((hidden, tall), down_map)],
            out_specs=[pl.BlockSpec((tokens, tall), lambda j, s: (0, jnp.minimum(j, half_steps - 1)))] * units
            + [pl.BlockSpec((tokens, tall), lambda j, s: (0, jnp.maximum(j - half_steps, 0)))] * units,
            scratch_shapes=[pltpu.VMEM((rows, tall), jnp.bfloat16)],
        ),
        compiler_params=pltpu.CompilerParams(dimension_semantics=("arbitrary",)),
        cost_estimate=pl.CostEstimate(
            flops=4 * rows * hidden * width,
            bytes_accessed=4 * hidden * width + 4 * units * tokens * width,
            transcendentals=0,
        ),
        name="ffn_down",
    )(side, put, hidden_rows, w_down)
    return results[:units], results[units:]


def slot_positions(ids, capacity, experts):
    flat = ids.reshape(-1)
    marks = (flat[:, None] == jnp.arange(experts, dtype=jnp.int32)[None, :]).astype(jnp.int32)
    before = jnp.cumsum(marks, axis=0) - marks
    slot = jnp.sum(before * marks, axis=1)
    return (flat * capacity + slot).reshape(ids.shape)


def exchange_body(tokens, exponents, expert_ids, affinity, w_gate, w_up, w_down):
    tok_rows, width = tokens.shape
    tile_count = width // 128
    top_count = expert_ids.shape[1]
    section_count = lax.axis_size("section")
    expert_count = lax.axis_size("expert")
    capacity = min(tok_rows, tok_rows * top_count * 5 // (4 * expert_count))
    slot_total = expert_count * capacity
    scales = jnp.exp2(exponents.astype(jnp.float32))
    tiles = tokens.astype(jnp.float32).reshape(tok_rows, tile_count, 128) / scales[:, :, None]
    quant = jnp.clip(tiles, -quant_limit, quant_limit).astype(jnp.bfloat16).reshape(tok_rows, width)
    slot_index = slot_positions(expert_ids, capacity, expert_count)
    columns = jnp.arange(slot_total, dtype=jnp.int32)
    select = jnp.any(slot_index[:, :, None] == columns[None, None, :], axis=1)
    contract = (((0,), (0,)), ((), ()))
    send_tiles = lax.dot_general(
        select.astype(jnp.bfloat16), quant, contract, preferred_element_type=jnp.float32
    ).astype(jnp.bfloat16)
    send_scales = lax.dot_general(
        select.astype(jnp.float32), scales, contract, precision=lax.Precision.HIGHEST
    ).astype(jnp.bfloat16)
    got_tiles, got_scales = (
        lax.all_to_all(
            send_tiles.reshape(expert_count, capacity, width),
            "expert",
            split_axis=0,
            concat_axis=0,
            tiled=True,
        ),
        lax.all_to_all(
            send_scales.reshape(expert_count, capacity, tile_count),
            "expert",
            split_axis=0,
            concat_axis=0,
            tiled=True,
        ),
    )
    all_tiles, all_scales = (
        lax.all_gather(got_tiles[None], "section", axis=0, tiled=True),
        lax.all_gather(got_scales[None], "section", axis=0, tiled=True),
    )
    restored = (
        all_tiles.reshape(section_count, expert_count, capacity, tile_count, 128)
        * all_scales[..., None]
    ).reshape(section_count, slot_total, width)
    hidden_local = w_gate.shape[2]
    gate = jnp.einsum(
        "srd,sdf->rf",
        restored,
        w_gate[0].reshape(section_count, width, hidden_local),
        preferred_element_type=jnp.float32,
    )
    up = jnp.einsum(
        "srd,sdf->rf",
        restored,
        w_up[0].reshape(section_count, width, hidden_local),
        preferred_element_type=jnp.float32,
    )
    hidden = (jax.nn.silu(gate) * up).astype(jnp.bfloat16)
    partial_rows = jnp.einsum(
        "rf,fsd->srd",
        hidden,
        w_down[0].reshape(hidden_local, section_count, width),
        preferred_element_type=jnp.float32,
    ).astype(jnp.bfloat16)
    summed = lax.psum_scatter(partial_rows, "section", scatter_dimension=0, tiled=True).astype(
        jnp.float32
    )
    summed_rows = summed.astype(jnp.bfloat16).reshape(expert_count, capacity, width)
    expert_rows = lax.all_to_all(summed_rows, "expert", split_axis=0, concat_axis=0, tiled=True)
    flat_rows = expert_rows.reshape(slot_total, width)
    picked = jnp.take(flat_rows, slot_index, axis=0)
    route_weight = route_scaling * affinity / jnp.sum(affinity, axis=1, keepdims=True)
    total = jnp.sum(picked.astype(jnp.float32) * route_weight[:, :, None], axis=1)
    return total.astype(jnp.bfloat16)


def pairs(size, flip):
    return [(index, index ^ flip) for index in range(size)]


def joined(*terms):
    total = terms[0].astype(jnp.float32)
    for term in terms[1:]:
        total += term.astype(jnp.float32)
    return total.astype(jnp.bfloat16)


def after(value, *deps):
    return lax.optimization_barrier((value, *deps))[0] if deps else value


def routing_table(expert_ids, affinity, experts):
    weight = route_scaling * affinity / jnp.sum(affinity, axis=1, keepdims=True)
    chosen = expert_ids[:, :, None] == jnp.arange(experts, dtype=jnp.int32)[None, None, :]
    table = jnp.sum(jnp.where(chosen, weight[:, :, None], 0.0), axis=1).T
    return lax.all_to_all(table, "expert", split_axis=0, concat_axis=0, tiled=True)


def routing_slots(table, places, capacity):
    me = lax.axis_index("expert")
    table = jnp.take(table, me ^ jnp.array(places, jnp.int32), axis=0)
    named = table > 0
    count = table.shape[1]
    ordered = jnp.arange(count)[:, None] <= jnp.arange(count)[None, :]
    slot = jnp.dot(
        named.astype(jnp.bfloat16), ordered.astype(jnp.bfloat16), preferred_element_type=jnp.float32
    ).astype(jnp.int32) - 1
    slot = jnp.where(named, slot, -1)
    hits = slot[:, None, :] == jnp.arange(capacity, dtype=jnp.int32)[None, :, None]
    slot_weight = jnp.sum(jnp.where(hits, table[:, None, :], 0.0), axis=2)
    put = slot[:, :, None] == jnp.arange(capacity, dtype=jnp.int32)[None, None, :]
    return hits.astype(jnp.bfloat16), put.astype(jnp.bfloat16), slot_weight.reshape(-1, 1)


def grid_body(tokens, exponents, expert_ids, affinity, w_gate, w_up, w_down):
    tok_rows, width = tokens.shape
    experts = lax.axis_size("expert")
    sections = lax.axis_size("section")
    capacity = min(tok_rows, tok_rows * expert_ids.shape[1] * 5 // (4 * experts))
    core_bit, x_bit, near_bit, far_bit = 1, 2, 4, 8

    def over(flip):
        return lambda value: lax.ppermute(value, "expert", pairs(experts, flip))

    core, cross_x, near, far = over(core_bit), over(x_bit), over(near_bit), over(far_bit)

    def cross_y(value):
        return lax.ppermute(value, "section", pairs(sections, 1))

    side = lax.axis_index("section").astype(jnp.int32).reshape(1)
    table = routing_table(expert_ids, affinity, experts)
    own, at_x, at_y, at_xy = ([[None, None] for _ in range(4)] for _ in range(4))

    def swap(*slots):
        for slot in slots:
            slot[1] = core(slot[0])

    def expert_up(quarter, mine, theirs, ks, *deps):
        near_rows = [rows for k in ks for rows in mine[k]]
        far_rows = [rows for k in ks for rows in theirs[k]]
        near_rows[0] = after(near_rows[0], *deps)
        return ffn_up(quarter, side, pick, slot_weight, near_rows, far_rows, w_gate[0], w_up[0])

    def expert_down(quarter, hidden_rows, *deps):
        return ffn_down(quarter, side, put, after(hidden_rows, *deps), w_down[0], width)

    def merge(outs, *deps):
        swapped = [[core(half[2 * n + 1]) for n in range(2)] for half in outs]
        return [
            [joined(after(half[2 * n], *deps), there[n]) for n in range(2)]
            for half, there in zip(outs, swapped)
        ]

    def go(hop, value, *deps):
        return hop(after(value, *deps))

    own[0][0] = restore(tokens, jnp.exp2(exponents.astype(jnp.float32)))
    own[1][0] = near(own[0][0])
    at_x[0][0], at_y[0][0] = cross_x(own[0][0]), cross_y(own[0][0])
    swap(own[0])
    own[1][0], at_x[0][0], at_y[0][0], table = lax.optimization_barrier(
        (own[1][0], at_x[0][0], at_y[0][0], table)
    )
    own[2][0] = go(far, own[0][0], own[1][0])
    at_x[1][0], at_y[1][0] = go(cross_x, own[1][0]), go(cross_y, own[1][0])
    swap(own[1], at_x[0], at_y[0])
    places = [
        flip ^ (k * near_bit) ^ plane
        for ks in ((0, 1), (2, 3))
        for flip in (0, x_bit)
        for k in ks
        for plane in (0, core_bit)
    ]
    pick, put, slot_weight = routing_slots(table, places, capacity)
    at_xy[0][0] = go(cross_x, at_y[0][0], at_x[1][0], put)
    at_xy[1][0] = go(cross_y, at_x[1][0], at_y[1][0])
    swap(at_y[1], at_x[1])
    sum_own, sum_x, sum_y, sum_xy, from_xy = ([None] * 4 for _ in range(5))

    hidden_own = expert_up(0, own, at_y, (0, 1))
    own[2][0] = after(own[2][0], hidden_own)
    own[3][0] = go(near, own[2][0])
    at_x[2][0], at_y[2][0] = go(cross_x, own[2][0]), go(cross_y, own[2][0])
    swap(own[2], at_xy[0], at_xy[1])
    hidden_x = expert_up(1, at_x, at_xy, (0, 1))
    own[3][0] = after(own[3][0], hidden_x)
    at_x[3][0], at_y[3][0] = go(cross_x, own[3][0]), go(cross_y, own[3][0])
    swap(own[3], at_x[2], at_y[2])
    outs_own = expert_down(0, hidden_own, hidden_x)
    outs_x = expert_down(1, hidden_x, outs_own[1][0])
    at_xy[2][0] = go(cross_x, at_y[2][0], at_x[3][0])
    at_xy[3][0] = go(cross_y, at_x[3][0], at_y[3][0])
    swap(at_x[3], at_y[3])
    at_xy[2][1], at_xy[3][1] = go(core, at_xy[2][0]), go(core, at_xy[3][0])

    hidden_own = expert_up(2, own, at_y, (2, 3), outs_x[1][0])
    sum_own[0:2], sum_y[0:2] = merge(outs_own, hidden_own)
    sum_x[0:2], sum_xy[0:2] = merge(outs_x, hidden_own)
    from_xy[0] = go(cross_x, sum_xy[0], hidden_own, at_xy[2][0])
    from_xy[1] = go(cross_y, sum_xy[1], hidden_own, at_xy[3][0])
    outs_own = expert_down(2, hidden_own)

    hidden_x = expert_up(3, at_x, at_xy, (2, 3), outs_own[1][0])
    sum_own[2:4], sum_y[2:4] = merge(outs_own, hidden_x)
    sum_y[0] = joined(sum_y[0], from_xy[0])
    sum_x[1] = joined(sum_x[1], from_xy[1])
    from_x1 = go(cross_x, sum_x[1], hidden_x)
    from_y3 = go(cross_y, sum_y[3], hidden_x)
    outs = expert_down(3, hidden_x)
    sum_x[2:4], sum_xy[2:4] = merge(outs)

    from_xy[2] = go(cross_x, sum_xy[2], from_x1)
    from_xy[3] = go(cross_y, sum_xy[3], from_y3)
    sum_y[2] = joined(sum_y[2], from_xy[2])
    sum_x[3] = joined(sum_x[3], from_xy[3])
    from_y1 = go(cross_y, sum_y[1], from_xy[3])
    sum_own[3] = joined(sum_own[3], cross_x(sum_x[3]), from_y3)
    sum_own[1] = joined(sum_own[1], from_x1, from_y1)
    sum_x[2], sum_y[2], _ = lax.optimization_barrier((sum_x[2], sum_y[2], sum_own[3]))
    from_near3 = near(sum_own[3])
    from_x2, from_y2 = cross_x(sum_x[2]), cross_y(sum_y[2])
    sum_own[2] = joined(sum_own[2], from_x2, from_y2, from_near3)
    from_far2 = far(sum_own[2])
    from_near1 = near(after(sum_own[1], from_near3))
    sum_x[0], sum_y[0], _ = lax.optimization_barrier((sum_x[0], sum_y[0], sum_own[2]))
    return joined(sum_own[0], cross_x(sum_x[0]), cross_y(sum_y[0]), from_near1, from_far2)


def solution(mesh):
    small = mesh.shape["section"] == 2 and mesh.shape["expert"] == 16

    def body(*operands):
        return (grid_body if small else exchange_body)(*operands)

    return jax.shard_map(
        body,
        mesh=mesh,
        in_specs=(
            P("expert", "section"),
            P("expert", "section"),
            P("expert", None),
            P("expert", None),
            P("expert", None, "section"),
            P("expert", None, "section"),
            P("expert", "section", None),
        ),
        out_specs=P("expert", "section"),
        check_vma=False,
    )
```
